32 devices in a mesh: dp: 16 (over z, y, core), shard: 2 (over x).
Axes of the slice: x: 2, y: 2, z: 4, core: 2. Of those that a mesh axis runs over, the one named last changes fastest.
Arguments:
- block_input: bfloat16 [4096, 1024], P(('dp', 'shard'))
- out_cotangent: bfloat16 [4096, 1024], P(('dp', 'shard')), may hold values from -6 to 6
- weight_input: float32 [1024, 3072], P('shard', 'dp'), may hold values from -0.1875 to 0.1875
- weight_output: float32 [1024, 1024], P('shard', 'dp'), may hold values from -0.1875 to 0.1875
- weight_gate: float32 [1024, 4608], P('shard', 'dp'), may hold values from -0.1875 to 0.1875
- weight_up: float32 [1024, 4608], P('shard', 'dp'), may hold values from -0.1875 to 0.1875
- weight_down: float32 [4608, 1024], P('shard', 'dp'), may hold values from -0.09375 to 0.09375
- conv_taps: float32 [3, 1024], P(None, 'shard'), may hold values from -3.5 to 3.5
- norm_gains: float32 [2, 1024], P(None, 'shard'), may hold values from 0.5 to 1.5
- first_input: float32 [1024, 3072], P('shard', 'dp'), may hold values from -20 to 20
- first_output: float32 [1024, 1024], P('shard', 'dp'), may hold values from -20 to 20
- first_gate: float32 [1024, 4608], P('shard', 'dp'), may hold values from -20 to 20
- first_up: float32 [1024, 4608], P('shard', 'dp'), may hold values from -20 to 20
- first_down: float32 [4608, 1024], P('shard', 'dp'), may hold values from -20 to 20
- first_taps: float32 [3, 1024], P(None, 'shard'), may hold values from -20 to 20
- first_gains: float32 [2, 1024], P(None, 'shard'), may hold values from -20 to 20
- second_input: float32 [1024, 3072], P('shard', 'dp'), may hold values from 20.48 to 122.88
- second_output: float32 [1024, 1024], P('shard', 'dp'), may hold values from 20.48 to 122.88
- second_gate: float32 [1024, 4608], P('shard', 'dp'), may hold values from 20.48 to 122.88
- second_up: float32 [1024, 4608], P('shard', 'dp'), may hold values from 20.48 to 122.88
- second_down: float32 [4608, 1024], P('shard', 'dp'), may hold values from 20.48 to 122.88
- second_taps: float32 [3, 1024], P(None, 'shard'), may hold values from 20.48 to 122.88
- second_gains: float32 [2, 1024], P(None, 'shard'), may hold values from 20.48 to 122.88
Outputs:
- block_output: bfloat16 [4096, 1024], P(('dp', 'shard'))
- input_gradient: float32 [4096, 1024], P(('dp', 'shard'))
- gradient_input: float32 [1024, 3072], P('shard', 'dp')
- gradient_output: float32 [1024, 1024], P('shard', 'dp')
- gradient_gate: float32 [1024, 4608], P('shard', 'dp')
- gradient_up: float32 [1024, 4608], P('shard', 'dp')
- gradient_down: float32 [4608, 1024], P('shard', 'dp')
- gradient_taps: float32 [3, 1024], P(None, 'shard')
- gradient_gains: float32 [2, 1024], P(None, 'shard')
- updated_input: float32 [1024, 3072], P('shard', 'dp')
- updated_output: float32 [1024, 1024], P('shard', 'dp')
- updated_gate: float32 [1024, 4608], P('shard', 'dp')
- updated_up: float32 [1024, 4608], P('shard', 'dp')
- updated_down: float32 [4608, 1024], P('shard', 'dp')
- updated_taps: float32 [3, 1024], P(None, 'shard')
- updated_gains: float32 [2, 1024], P(None, 'shard')
- moment_input: float32 [1024, 3072], P('shard', 'dp')
- moment_output: float32 [1024, 1024], P('shard', 'dp')
- moment_gate: float32 [1024, 4608], P('shard', 'dp')
- moment_up: float32 [1024, 4608], P('shard', 'dp')
- moment_down: float32 [4608, 1024], P('shard', 'dp')
- moment_taps: float32 [3, 1024], P(None, 'shard')
- moment_gains: float32 [2, 1024], P(None, 'shard')
- square_input: float32 [1024, 3072], P('shard', 'dp')
- square_output: float32 [1024, 1024], P('shard', 'dp')
- square_gate: float32 [1024, 4608], P('shard', 'dp')
- square_up: float32 [1024, 4608], P('shard', 'dp')
- square_down: float32 [4608, 1024], P('shard', 'dp')
- square_taps: float32 [3, 1024], P(None, 'shard')
- square_gains: float32 [2, 1024], P(None, 'shard')
The draws below stay inside these ranges and needn't reach their ends.
All inputs are finite; a program needn't handle non-finite values.
Results may differ from the reference program's by a relative error of at most 0.00435.
The reference program's roundings to bfloat16 on the way count: a program that leaves them out, or rounds other values in their place, can miss the bound.
Values may be sent and summed in bfloat16 or wider, within the bound.
No kernel may reach another device: no remote copies, remote signals or barrier semaphores. Data moves between devices by JAX's collectives and lax.ppermute only.
A program may use at most 320 MiB of HBM per device.

```python
import math
import jax
import jax.numpy as jnp
from jax import lax

D = 1024
FF = 4608
KCONV = 3
LEN = 128
STEP = 10
TOKENS = 4096


def draw_block_input(key, part):
    base_key = jax.random.fold_in(key, 11)
    column_key = jax.random.fold_in(key, 12)
    row_key = jax.random.fold_in(key, 13)
    base = jax.random.normal(base_key, (TOKENS, D), jnp.float32)
    columns = jnp.exp(jax.random.uniform(column_key, (1, D), jnp.float32, -1.15, 1.15))
    rows = jnp.exp(jax.random.uniform(row_key, (TOKENS, 1), jnp.float32, -1.15, 1.15))
    return (base * columns * rows).astype(jnp.bfloat16)


def strengthened(entries, rng, source, target, shards_of, factor):
    owner, partner = [(jnp.arange(entries.shape[position]) // (entries.shape[position] // shards_of)).reshape([-1 if axis == position else 1 for axis in range(entries.ndim)]) for position in (source, target)]
    chosen = jax.random.permutation(rng, shards_of)[partner]
    strong = (owner == chosen) | (owner == (partner + shards_of // 2) % shards_of)
    return jnp.where(strong, factor * entries, entries)


def block_scale(rng, shape, cuts, smallest, high):
    def one(dim, shards_of):
        heights = jax.random.uniform(jax.random.fold_in(jax.random.fold_in(rng, 6), dim), (shards_of,), jnp.float32, smallest / len(cuts), high / len(cuts))
        return jnp.repeat(jnp.exp(heights), shape[dim] // shards_of).reshape((-1,) + (1,) * (len(shape) - dim - 1))

    loudness = one(*cuts[0])
    for cut in cuts[1:]:
        loudness = loudness * one(*cut)
    return loudness


def bell_draw(key, shape, scale, bound, pieces=(), kind=jnp.bfloat16):
    values = jax.random.normal(key, shape, jnp.float32) * scale
    if len(pieces) > 0:
        values = block_scale(key, shape, pieces, -0.22, 0.18) * values
    return jnp.clip(values, min=-bound, max=bound).astype(kind)


def heavy_noise(rng, dims, width, reach, cuts, heavy, kind=jnp.bfloat16):
    values = width * jax.random.normal(rng, dims, jnp.float32)
    if cuts:
        values = values * block_scale(rng, dims, cuts, -0.22, 0.18)
    return jnp.clip(strengthened(values, jax.random.fold_in(rng, 3), *heavy), -reach, reach).astype(kind)


def setup_inputs(seed: int = 0) -> dict:
    streams_of = jax.random.split(jax.random.key(seed), 24)
    block_input = draw_block_input(jax.random.fold_in(streams_of[23], 71), 0)
    out_cotangent = heavy_noise(streams_of[1], (TOKENS, D), 1.0, 6.0, ((0, 32),), (0, 1, 32, 2.75))
    weight_input = bell_draw(streams_of[2], (D, 3 * D), D ** -0.5, 0.1875, ((0, 2), (1, 16)), jnp.float32)
    weight_output = bell_draw(streams_of[3], (D, D), D ** -0.5, 0.1875, ((0, 2), (1, 16)), jnp.float32)
    weight_gate = bell_draw(streams_of[4], (D, FF), D ** -0.5, 0.1875, ((0, 2), (1, 16)), jnp.float32)
    weight_up = bell_draw(streams_of[5], (D, FF), D ** -0.5, 0.1875, ((0, 2), (1, 16)), jnp.float32)
    weight_down = bell_draw(streams_of[6], (FF, D), FF ** -0.5, 0.09375, ((0, 2), (1, 16)), jnp.float32)
    conv_taps = bell_draw(streams_of[7], (KCONV, D), KCONV ** -0.5, 3.5, ((1, 2),), jnp.float32)
    norm_gains = jnp.clip(1.0 + 0.1 * jax.random.normal(streams_of[8], (2, D), jnp.float32), 0.5, 1.5)
    first_input = bell_draw(streams_of[9], (D, 3 * D), (0.05 * TOKENS ** 0.5), 20.0, ((0, 2), (1, 16)), jnp.float32)
    first_output = bell_draw(streams_of[10], (D, D), (0.05 * TOKENS ** 0.5), 20.0, ((0, 2), (1, 16)), jnp.float32)
    first_gate = bell_draw(streams_of[11], (D, FF), (0.05 * TOKENS ** 0.5), 20.0, ((0, 2), (1, 16)), jnp.float32)
    first_up = bell_draw(streams_of[12], (D, FF), (0.05 * TOKENS ** 0.5), 20.0, ((0, 2), (1, 16)), jnp.float32)
    first_down = bell_draw(streams_of[13], (FF, D), (0.05 * TOKENS ** 0.5), 20.0, ((0, 2), (1, 16)), jnp.float32)
    first_taps = bell_draw(streams_of[14], (KCONV, D), (0.05 * TOKENS ** 0.5), 20.0, ((1, 2),), jnp.float32)
    first_gains = bell_draw(streams_of[15], (2, D), (0.05 * TOKENS ** 0.5), 20.0, ((1, 2),), jnp.float32)
    second_input = jnp.clip(jnp.exp(math.log(122.88) - 1.7917595 * jax.random.uniform(streams_of[16], (D, 3 * D), jnp.float32) ** block_scale(streams_of[16], (D, 3 * D), ((0, 2), (1, 16)), -0.2, 0.2)), 20.48, 122.88)
    second_output = jnp.clip(jnp.exp(math.log(122.88) - 1.7917595 * jax.random.uniform(streams_of[17], (D, D), jnp.float32) ** block_scale(streams_of[17], (D, D), ((0, 2), (1, 16)), -0.2, 0.2)), 20.48, 122.88)
    second_gate = jnp.clip(jnp.exp(math.log(122.88) - 1.7917595 * jax.random.uniform(streams_of[18], (D, FF), jnp.float32) ** block_scale(streams_of[18], (D, FF), ((0, 2), (1, 16)), -0.2, 0.2)), 20.48, 122.88)
    second_up = jnp.clip(jnp.exp(math.log(122.88) - 1.7917595 * jax.random.uniform(streams_of[19], (D, FF), jnp.float32) ** block_scale(streams_of[19], (D, FF), ((0, 2), (1, 16)), -0.2, 0.2)), 20.48, 122.88)
    second_down = jnp.clip(jnp.exp(math.log(122.88) - 1.7917595 * jax.random.uniform(streams_of[20], (FF, D), jnp.float32) ** block_scale(streams_of[20], (FF, D), ((0, 2), (1, 16)), -0.2, 0.2)), 20.48, 122.88)
    second_taps = jnp.clip(jnp.exp(math.log(122.88) - 1.7917595 * jax.random.uniform(streams_of[21], (KCONV, D), jnp.float32) ** block_scale(streams_of[21], (KCONV, D), ((1, 2),), -0.2, 0.2)), 20.48, 122.88)
    second_gains = jnp.clip(jnp.exp(math.log(122.88) - 1.7917595 * jax.random.uniform(streams_of[22], (2, D), jnp.float32) ** block_scale(streams_of[22], (2, D), ((1, 2),), -0.2, 0.2)), 20.48, 122.88)
    return dict(block_input=block_input, out_cotangent=out_cotangent, weight_input=weight_input, weight_output=weight_output, weight_gate=weight_gate, weight_up=weight_up, weight_down=weight_down, conv_taps=conv_taps, norm_gains=norm_gains, first_input=first_input, first_output=first_output, first_gate=first_gate, first_up=first_up, first_down=first_down, first_taps=first_taps, first_gains=first_gains, second_input=second_input, second_output=second_output, second_gate=second_gate, second_up=second_up, second_down=second_down, second_taps=second_taps, second_gains=second_gains)


epsilon_norm = 1e-05
epsilon_adam = 1e-08
beta_first = 0.9
beta_second = 0.95
rate_matrix = 0.01
rate_vector = 0.1
weight_decay = 0.1

def product(left, right):
    return jnp.dot(left, right, preferred_element_type=jnp.float32)

def times_transposed(left, right):
    return lax.dot_general(left, right, (((1,), (1,)), ((), ())), preferred_element_type=jnp.float32)

def transposed_times(left, right):
    return lax.dot_general(left, right, (((0,), (0,)), ((), ())), preferred_element_type=jnp.float32)

def delayed(values, steps):
    seqs = values.reshape(-1, LEN, values.shape[-1])
    padded = jnp.pad(seqs, ((0, 0), (steps, 0), (0, 0)))[:, :LEN]
    return padded.reshape(values.shape)

def advanced(values, steps):
    seqs = values.reshape(-1, LEN, values.shape[-1])
    padded = jnp.pad(seqs, ((0, 0), (0, steps), (0, 0)))[:, steps:]
    return padded.reshape(values.shape)

def norm_scale(values):
    return lax.rsqrt(lax.optimization_barrier(jnp.mean(values * values, axis=1, keepdims=True)) + epsilon_norm)

def norm_back(grad_in, normed, scale, gain):
    weighted = grad_in * gain
    return scale * (weighted - normed * lax.optimization_barrier(jnp.mean(weighted * normed, axis=1, keepdims=True)))

def layer_pass(inputs, cotangent, whole_input, whole_output, whole_gate, whole_up, whole_down, whole_taps, whole_gains):
    values = inputs.astype(jnp.float32)
    gains = whole_gains.astype(jnp.float32)
    taps = whole_taps.astype(jnp.float32)
    scale_one = norm_scale(values)
    normed_one = values * scale_one
    hidden_one = (normed_one * gains[0]).astype(jnp.bfloat16)
    projected = product(hidden_one, whole_input)
    input_gate = projected[:, :D]
    output_gate = projected[:, D:2 * D]
    mixer_values = projected[:, 2 * D:]
    mixed_in = input_gate * mixer_values
    shifted = [delayed(mixed_in, step) for step in range(KCONV)]
    conv_out = taps[0] * shifted[0]
    for step in range(1, KCONV):
        conv_out = conv_out + taps[step] * shifted[step]
    gated = (output_gate * conv_out).astype(jnp.bfloat16)
    residual = values + product(gated, whole_output)
    scale_two = norm_scale(residual)
    normed_two = residual * scale_two
    hidden_two = (normed_two * gains[1]).astype(jnp.bfloat16)
    gate_pre = product(hidden_two, whole_gate)
    up_pre = product(hidden_two, whole_up)
    sigmoid_gate = jax.nn.sigmoid(gate_pre)
    silu_gate = gate_pre * sigmoid_gate
    activated = (silu_gate * up_pre).astype(jnp.bfloat16)
    block_output = (residual + product(activated, whole_down)).astype(jnp.bfloat16)
    act_grad = times_transposed(cotangent, whole_down)
    gate_grad = (act_grad * up_pre * sigmoid_gate * (1.0 + gate_pre * (1.0 - sigmoid_gate))).astype(jnp.bfloat16)
    up_grad = (act_grad * silu_gate).astype(jnp.bfloat16)
    hidden_two_grad = times_transposed(gate_grad, whole_gate) + times_transposed(up_grad, whole_up)
    gain_two_grad = lax.optimization_barrier(jnp.sum(hidden_two_grad * normed_two, axis=0))
    residual_grad = cotangent.astype(jnp.float32) + norm_back(hidden_two_grad, normed_two, scale_two, gains[1])
    residual_half = residual_grad.astype(jnp.bfloat16)
    gated_grad = times_transposed(residual_half, whole_output)
    conv_grad = gated_grad * output_gate
    mixed_grad = taps[0] * conv_grad
    for step in range(1, KCONV):
        mixed_grad = mixed_grad + taps[step] * advanced(conv_grad, step)
    taps_grad = jnp.stack([lax.optimization_barrier(jnp.sum(conv_grad * shifted[step], axis=0)) for step in range(KCONV)], 0)
    projected_grad = jnp.concatenate([mixed_grad * mixer_values, gated_grad * conv_out, mixed_grad * input_gate], axis=1).astype(jnp.bfloat16)
    hidden_one_grad = times_transposed(projected_grad, whole_input)
    gain_one_grad = lax.optimization_barrier(jnp.sum(hidden_one_grad * normed_one, axis=0))
    input_gradient = residual_grad + norm_back(hidden_one_grad, normed_one, scale_one, gains[0])
    pairs = ((hidden_one, projected_grad), (gated, residual_half), (hidden_two, gate_grad), (hidden_two, up_grad), (activated, cotangent))
    gains_grad = jnp.stack([gain_one_grad, gain_two_grad], 0)
    return (block_output, input_gradient, pairs, taps_grad, gains_grad)

def adam_step(param, grad, moment, square, rate, decay):
    moment_new = beta_first * moment + (1.0 - beta_first) * grad
    square_new = beta_second * square + (1.0 - beta_second) * grad * grad
    corrected = moment_new / (1.0 - beta_first ** STEP)
    spread = jnp.sqrt(square_new / (1.0 - beta_second ** STEP))
    updated = param - rate * (corrected / (spread + epsilon_adam) + decay * param)
    return (updated, moment_new, square_new)

def reference(block_input, out_cotangent, weight_input, weight_output, weight_gate, weight_up, weight_down, conv_taps, norm_gains, first_input, first_output, first_gate, first_up, first_down, first_taps, first_gains, second_input, second_output, second_gate, second_up, second_down, second_taps, second_gains):
    params = (weight_input, weight_output, weight_gate, weight_up, weight_down, conv_taps, norm_gains)
    halves = tuple((param.astype(jnp.bfloat16) for param in params))
    total_rows = block_input.shape[0]
    seq_total = total_rows // LEN
    per_block = math.gcd(seq_total, max(1, 4096 // LEN))
    block_rows = per_block * LEN
    blocks = total_rows // block_rows
    inputs = block_input.reshape(blocks, block_rows, D)
    cotangents = out_cotangent.reshape(blocks, block_rows, D)
    zeros = tuple((jnp.zeros(param.shape, jnp.float32) for param in params))

    def visit(carry, pair):
        output, in_grad, pairs, taps_grad, gains_grad = layer_pass(pair[0], pair[1], *halves)
        terms = tuple((transposed_times(left, right) for left, right in pairs)) + (taps_grad, gains_grad)
        return (tuple((total + term for total, term in zip(carry, terms))), (output, in_grad))
    grads, (outputs, in_grads) = lax.scan(visit, zeros, (inputs, cotangents))
    firsts = (first_input, first_output, first_gate, first_up, first_down, first_taps, first_gains)
    seconds = (second_input, second_output, second_gate, second_up, second_down, second_taps, second_gains)
    updated = []
    moments = []
    squares = []
    for index in range(7):
        rate = rate_matrix if index < 5 else rate_vector
        decay = weight_decay if index < 5 else 0.0
        result = adam_step(params[index], grads[index], firsts[index], seconds[index], rate, decay)
        updated.append(result[0])
        moments.append(result[1])
        squares.append(result[2])
    return (outputs.reshape(total_rows, D), in_grads.reshape(total_rows, D), grads[0], grads[1], grads[2], grads[3], grads[4], grads[5], grads[6], updated[0], updated[1], updated[2], updated[3], updated[4], updated[5], updated[6], moments[0], moments[1], moments[2], moments[3], moments[4], moments[5], moments[6], squares[0], squares[1], squares[2], squares[3], squares[4], squares[5], squares[6])
```

```python
import jax
import jax.numpy as jnp
from jax import lax
from jax.sharding import Mesh
from jax.sharding import PartitionSpec as P

KCONV = 3
LEN = 128
STEP = 10


epsilon_norm = 1e-05
epsilon_adam = 1e-08
beta_first = 0.9
beta_second = 0.95
rate_matrix = 0.01
rate_vector = 0.1
weight_decay = 0.1


def product(left, right):
    return jnp.dot(left, right, preferred_element_type=jnp.float32)


def times_transposed(left, right):
    return lax.dot_general(
        left, right, (((1,), (1,)), ((), ())), preferred_element_type=jnp.float32
    )


def transposed_times(left, right):
    return lax.dot_general(
        left, right, (((0,), (0,)), ((), ())), preferred_element_type=jnp.float32
    )


def delayed(values, steps):
    seqs = values.reshape(-1, LEN, values.shape[-1])
    padded = jnp.pad(seqs, ((0, 0), (steps, 0), (0, 0)))[:, :LEN]
    return padded.reshape(values.shape)


def advanced(values, steps):
    seqs = values.reshape(-1, LEN, values.shape[-1])
    padded = jnp.pad(seqs, ((0, 0), (0, steps), (0, 0)))[:, steps:]
    return padded.reshape(values.shape)


def norm_scale(values):
    return lax.rsqrt(jnp.mean(values * values, axis=1, keepdims=True) + epsilon_norm)


def norm_back(grad_in, normed, scale, gain):
    weighted = grad_in * gain
    return scale * (weighted - normed * jnp.mean(weighted * normed, axis=1, keepdims=True))


DP = ("a", "b", "core")
TEAM = ("b", "x")
POOL = ("a", "core")
ALL = ("a", "b", "core", "x")


def team_gather(values):
    count = lax.axis_size("b") * lax.axis_size("x")
    blocks = [values]
    for k in range(1, count):
        blocks.append(lax.ppermute(values, TEAM, [(i, i ^ k) for i in range(count)]))
    return jnp.concatenate(blocks, axis=0)


def team_sum(partial):
    count = lax.axis_size("b") * lax.axis_size("x")
    blocks = partial.reshape(count, -1, partial.shape[-1])
    total = blocks[0]
    for k in range(1, count):
        sent = blocks[k].astype(jnp.bfloat16)
        total = total + lax.ppermute(sent, TEAM, [(i, i ^ k) for i in range(count)]).astype(
            jnp.float32
        )
    return total


def pool_sum(partial):
    count = lax.axis_size("a")
    blocks = partial.reshape(count, 2, -1, partial.shape[-1])
    core = lax.axis_index("core")
    mine = lax.dynamic_index_in_dim(blocks, core, 1, keepdims=False)
    other = lax.dynamic_index_in_dim(blocks, 1 - core, 1, keepdims=False)
    pair = mine + lax.ppermute(other, "core", [(0, 1), (1, 0)])
    place = lax.axis_index("a")
    total = lax.dynamic_index_in_dim(pair, place, 0, keepdims=False)
    for k in range(1, count):
        sent = lax.dynamic_index_in_dim(pair, place ^ k, 0, keepdims=False).astype(jnp.bfloat16)
        total = total + lax.ppermute(sent, "a", [(i, i ^ k) for i in range(count)]).astype(
            jnp.float32
        )
    return total


def pool_gather(block):
    return lax.all_gather(block, POOL, axis=0, tiled=True)


def row_blocks(parts):
    n, s = lax.axis_size(DP), lax.axis_size("x")
    joined = jnp.concatenate([part.reshape(n, -1, part.shape[-1]) for part in parts], axis=1)
    width = joined.shape[-1]
    moved = lax.all_to_all(joined, DP, 0, 0, tiled=True)
    whole = jnp.transpose(moved, (1, 0, 2)).reshape(-1, n * width)
    return lax.ppermute(whole, ALL, [(d * s + x, x * n + d) for d in range(n) for x in range(s)])


def row_blocks_back(block):
    n, s = lax.axis_size(DP), lax.axis_size("x")
    whole = lax.ppermute(block, ALL, [(x * n + d, d * s + x) for d in range(n) for x in range(s)])
    rows, width = whole.shape[0], whole.shape[1] // n
    pieces = jnp.transpose(whole.reshape(rows, n, width), (1, 0, 2))
    return lax.all_to_all(pieces, DP, 0, 0, tiled=True)


def triple_tables(n):
    block_of = [[0] * 3 for _ in range(n)]
    round_of = [[0] * 3 for _ in range(n)]
    for i in range(n):
        for r in range(3):
            block_of[(3 * i + r) % n][r] = (3 * i + r) // n
            round_of[(3 * i + r) % n][(3 * i + r) // n] = r
    return jnp.array(block_of, jnp.int32), jnp.array(round_of, jnp.int32)


def triple_blocks(weight):
    n = lax.axis_size(DP)
    granules = weight.T.reshape(3, -1, weight.shape[0])
    came = jnp.stack(
        [lax.ppermute(granules[r], DP, [(i, (3 * i + r) % n) for i in range(n)]) for r in range(3)]
    )
    order = triple_tables(n)[1][lax.axis_index(DP)]
    sorted_blocks = jnp.concatenate(
        [lax.dynamic_slice_in_dim(came, order[b], 1, 0) for b in range(3)], axis=0
    )
    return lax.all_to_all(sorted_blocks, "x", 1, 2, tiled=True)


def triple_blocks_back(grad):
    n = lax.axis_size(DP)
    blocks = lax.all_to_all(grad, "x", 2, 1, tiled=True)
    order = triple_tables(n)[0][lax.axis_index(DP)]
    granules = [
        lax.ppermute(
            lax.dynamic_index_in_dim(blocks, order[r], 0, keepdims=False),
            DP,
            [((3 * i + r) % n, i) for i in range(n)],
        )
        for r in range(3)
    ]
    return jnp.concatenate(granules, axis=0).T


def team_features(vector):
    a, b, x = lax.axis_size("a"), lax.axis_size("b"), lax.axis_size("x")
    split = vector.reshape(vector.shape[0], a, b, 2, x, -1)
    split = lax.dynamic_index_in_dim(split, lax.axis_index("b"), 2, keepdims=False)
    split = lax.dynamic_index_in_dim(split, lax.axis_index("x"), 3, keepdims=False)
    return split.reshape(vector.shape[0], -1)


def team_features_back(vector, width):
    a, b, x = lax.axis_size("a"), lax.axis_size("b"), lax.axis_size("x")
    rows = vector.shape[0]
    zeros = jnp.zeros((rows, a, b, 2, x, width // (a * b * 2 * x)), vector.dtype)
    split = vector.reshape(rows, a, 1, 2, 1, -1)
    place = (0, 0, lax.axis_index("b"), 0, lax.axis_index("x"), 0)
    return lax.dynamic_update_slice(zeros, split, place).reshape(rows, width)


def adam_step(param, grad, moment, square, rate, decay):
    moment_new = beta_first * moment + (1.0 - beta_first) * grad
    square_new = beta_second * square + (1.0 - beta_second) * grad * grad
    corrected = moment_new / (1.0 - beta_first**STEP)
    spread = jnp.sqrt(square_new / (1.0 - beta_second**STEP))
    updated = param - rate * (corrected / (spread + epsilon_adam) + decay * param)
    return (updated, moment_new, square_new)


def shards(
    block_input,
    out_cotangent,
    weight_input,
    weight_output,
    weight_gate,
    weight_up,
    weight_down,
    conv_taps,
    norm_gains,
    first_input,
    first_output,
    first_gate,
    first_up,
    first_down,
    first_taps,
    first_gains,
    second_input,
    second_output,
    second_gate,
    second_up,
    second_down,
    second_taps,
    second_gains,
):
    half = jnp.bfloat16
    width = block_input.shape[1]
    ff_rows = weight_down.shape[0] // lax.axis_size(DP)

    mix_in = triple_blocks(weight_input.astype(half))
    rows = row_blocks([weight_down.astype(half), weight_output.astype(half)])
    fan = lax.all_to_all(
        jnp.stack([weight_gate.astype(half).T, weight_up.astype(half).T]), "x", 1, 2, tiled=True
    )
    team_in = lax.all_gather(mix_in, POOL, axis=1, tiled=True)
    team_out = pool_gather(rows[ff_rows:])
    team_gate = pool_gather(fan[0])
    team_up = pool_gather(fan[1])
    team_down = pool_gather(rows[:ff_rows])
    vectors = lax.all_gather(
        jnp.concatenate([conv_taps, norm_gains], axis=0).astype(half), "x", axis=1, tiled=True
    ).astype(jnp.float32)
    gains = vectors[KCONV:]
    taps = team_features(vectors[:KCONV])

    values = block_input.astype(jnp.float32)
    cotangents = team_gather(out_cotangent)
    scale_one = norm_scale(values)
    normed_one = values * scale_one
    hidden_one = team_gather((normed_one * gains[0]).astype(half))
    input_gate = times_transposed(hidden_one, team_in[0])
    output_gate = times_transposed(hidden_one, team_in[1])
    mixer_values = times_transposed(hidden_one, team_in[2])
    mixed_in = input_gate * mixer_values
    shifted = [delayed(mixed_in, step) for step in range(KCONV)]
    conv_out = taps[0] * shifted[0]
    for step in range(1, KCONV):
        conv_out = conv_out + taps[step] * shifted[step]
    gated = (output_gate * conv_out).astype(half)
    residual = values + team_sum(product(gated, team_out))
    scale_two = norm_scale(residual)
    normed_two = residual * scale_two
    hidden_two = team_gather((normed_two * gains[1]).astype(half))
    gate_pre = times_transposed(hidden_two, team_gate)
    up_pre = times_transposed(hidden_two, team_up)
    act_grad = times_transposed(cotangents, team_down)
    sigmoid_gate = jax.nn.sigmoid(gate_pre)
    silu_gate = gate_pre * sigmoid_gate
    activated = (silu_gate * up_pre).astype(half)
    gate_grad = (act_grad * up_pre * sigmoid_gate * (1.0 + gate_pre * (1.0 - sigmoid_gate))).astype(
        half
    )
    up_grad = (act_grad * silu_gate).astype(half)
    hidden_two_grad = team_sum(product(gate_grad, team_gate) + product(up_grad, team_up))
    block_output = (residual + team_sum(product(activated, team_down))).astype(half)
    gain_two_grad = jnp.sum(hidden_two_grad * normed_two, axis=0)
    residual_grad = out_cotangent.astype(jnp.float32) + norm_back(
        hidden_two_grad, normed_two, scale_two, gains[1]
    )
    residual_half = team_gather(residual_grad.astype(half))
    own_down = pool_sum(transposed_times(activated, cotangents))
    own_gate = pool_sum(transposed_times(gate_grad, hidden_two))
    own_up = pool_sum(transposed_times(up_grad, hidden_two))
    gated_grad = times_transposed(residual_half, team_out)
    conv_grad = gated_grad * output_gate
    mixed_grad = taps[0] * conv_grad
    for step in range(1, KCONV):
        mixed_grad = mixed_grad + taps[step] * advanced(conv_grad, step)
    taps_grad = jnp.stack([jnp.sum(conv_grad * shifted[step], axis=0) for step in range(KCONV)], 0)
    projected_grad = [
        (mixed_grad * mixer_values).astype(half),
        (gated_grad * conv_out).astype(half),
        (mixed_grad * input_gate).astype(half),
    ]
    hidden_one_grad = team_sum(
        product(projected_grad[0], team_in[0])
        + product(projected_grad[1], team_in[1])
        + product(projected_grad[2], team_in[2])
    )
    pool = lax.axis_size(POOL)
    terms = jnp.concatenate(
        [transposed_times(grad, hidden_one).reshape(pool, -1, width) for grad in projected_grad]
        + [transposed_times(gated, residual_half).reshape(pool, -1, width)],
        axis=1,
    )
    own_mix = pool_sum(terms)
    mix_rows = own_mix.shape[0] // 4
    gain_one_grad = jnp.sum(hidden_one_grad * normed_one, axis=0)
    input_gradient = residual_grad + norm_back(hidden_one_grad, normed_one, scale_one, gains[0])
    vector_terms = jnp.concatenate(
        [team_features_back(taps_grad, width), gain_one_grad[None, :], gain_two_grad[None, :]],
        axis=0,
    )
    vector_all = lax.psum(vector_terms, ALL)
    owned = conv_taps.shape[1]
    vector_total = lax.dynamic_slice_in_dim(vector_all, lax.axis_index("x") * owned, owned, 1)
    grad_taps = vector_total[:KCONV]
    grad_gains = vector_total[KCONV:]

    grad_fan = lax.all_to_all(jnp.stack([own_gate, own_up]), "x", 2, 1, tiled=True)
    grad_gate = grad_fan[0].T
    grad_up = grad_fan[1].T
    grad_input = triple_blocks_back(own_mix[: 3 * mix_rows].reshape(3, mix_rows, width))
    grad_rows = row_blocks_back(jnp.concatenate([own_down, own_mix[3 * mix_rows :]], axis=0))
    grad_down = grad_rows[:, :ff_rows].reshape(weight_down.shape)
    grad_output = grad_rows[:, ff_rows:].reshape(weight_output.shape)
    params = (
        weight_input,
        weight_output,
        weight_gate,
        weight_up,
        weight_down,
        conv_taps,
        norm_gains,
    )
    grads = (grad_input, grad_output, grad_gate, grad_up, grad_down, grad_taps, grad_gains)
    firsts = (first_input, first_output, first_gate, first_up, first_down, first_taps, first_gains)
    seconds = (
        second_input,
        second_output,
        second_gate,
        second_up,
        second_down,
        second_taps,
        second_gains,
    )
    updated = []
    moments = []
    squares = []
    for index in range(7):
        rate = rate_matrix if index < 5 else rate_vector
        decay = weight_decay if index < 5 else 0.0
        result = adam_step(params[index], grads[index], firsts[index], seconds[index], rate, decay)
        updated.append(result[0])
        moments.append(result[1])
        squares.append(result[2])
    return (
        block_output,
        input_gradient,
        grads[0],
        grads[1],
        grads[2],
        grads[3],
        grads[4],
        grads[5],
        grads[6],
        updated[0],
        updated[1],
        updated[2],
        updated[3],
        updated[4],
        updated[5],
        updated[6],
        moments[0],
        moments[1],
        moments[2],
        moments[3],
        moments[4],
        moments[5],
        moments[6],
        squares[0],
        squares[1],
        squares[2],
        squares[3],
        squares[4],
        squares[5],
        squares[6],
    )


def solution(mesh):
    dp, shard = mesh.shape["dp"], mesh.shape["shard"]
    mesh = Mesh(mesh.devices.reshape(dp // 4, 2, 2, shard), ALL)
    placed = (
        P(ALL, None),
        P(ALL, None),
        P("x", DP),
        P("x", DP),
        P("x", DP),
        P("x", DP),
        P("x", DP),
        P(None, "x"),
        P(None, "x"),
        P("x", DP),
        P("x", DP),
        P("x", DP),
        P("x", DP),
        P("x", DP),
        P(None, "x"),
        P(None, "x"),
        P("x", DP),
        P("x", DP),
        P("x", DP),
        P("x", DP),
        P("x", DP),
        P(None, "x"),
        P(None, "x"),
    )
    return jax.shard_map(
        shards,
        mesh=mesh,
        in_specs=placed,
        out_specs=(
            P(ALL, None),
            P(ALL, None),
            P("x", DP),
            P("x", DP),
            P("x", DP),
            P("x", DP),
            P("x", DP),
            P(None, "x"),
            P(None, "x"),
            P("x", DP),
            P("x", DP),
            P("x", DP),
            P("x", DP),
            P("x", DP),
            P(None, "x"),
            P(None, "x"),
            P("x", DP),
            P("x", DP),
            P("x", DP),
            P("x", DP),
            P("x", DP),
            P(None, "x"),
            P(None, "x"),
            P("x", DP),
            P("x", DP),
            P("x", DP),
            P("x", DP),
            P("x", DP),
            P(None, "x"),
            P(None, "x"),
        ),
        check_vma=False,
    )
```

```python
import jax
import jax.numpy as jnp
from jax import lax
from jax.sharding import Mesh
from jax.sharding import PartitionSpec as P

KCONV = 3
LEN = 128
STEP = 10


epsilon_norm = 1e-05
epsilon_adam = 1e-08
beta_first = 0.9
beta_second = 0.95
rate_matrix = 0.01
rate_vector = 0.1
weight_decay = 0.1


def product(left, right):
    return jnp.dot(left, right, preferred_element_type=jnp.float32)


def times_transposed(left, right):
    return lax.dot_general(
        left, right, (((1,), (1,)), ((), ())), preferred_element_type=jnp.float32
    )


def transposed_times(left, right):
    return lax.dot_general(
        left, right, (((0,), (0,)), ((), ())), preferred_element_type=jnp.float32
    )


def delayed(values, steps):
    seqs = values.reshape(-1, LEN, values.shape[-1])
    padded = jnp.pad(seqs, ((0, 0), (steps, 0), (0, 0)))[:, :LEN]
    return padded.reshape(values.shape)


def advanced(values, steps):
    seqs = values.reshape(-1, LEN, values.shape[-1])
    padded = jnp.pad(seqs, ((0, 0), (0, steps), (0, 0)))[:, steps:]
    return padded.reshape(values.shape)


def norm_scale(values):
    return lax.rsqrt(jnp.mean(values * values, axis=1, keepdims=True) + epsilon_norm)


def norm_back(grad_in, normed, scale, gain):
    weighted = grad_in * gain
    return scale * (weighted - normed * jnp.mean(weighted * normed, axis=1, keepdims=True))


DP = ("a", "b", "core")
TEAM = ("b", "x")
ALL = ("a", "b", "core", "x")


def from_xor(values, axes, k):
    if k == 0:
        return values
    return lax.ppermute(values, axes, [(i, i ^ k) for i in range(lax.axis_size(axes))])


def pick(values, index, axis=0):
    return lax.dynamic_index_in_dim(values, index, axis, keepdims=False)


def team_gather(values):
    blocks = [from_xor(values, TEAM, k) for k in range(lax.axis_size(TEAM))]
    return jnp.concatenate(blocks, axis=0)


def team_sum(partial, wire):
    count = lax.axis_size(TEAM)
    blocks = partial.reshape(count, -1, partial.shape[-1])
    total = blocks[0]
    for k in range(1, count):
        total = total + from_xor(blocks[k].astype(wire), TEAM, k).astype(jnp.float32)
    return total


def pool_gather(block):
    count = lax.axis_size("a")
    found = []
    for d in range(count):
        if d > 0:
            block = lax.ppermute(block, "a", [(i, (i + 1) % count) for i in range(count)])
        found += [block, from_xor(block, "core", 1)]
    return found


def pool_sum(partial):
    count = lax.axis_size("a")
    blocks = partial.reshape(count, 2, -1, partial.shape[-1])
    pair = blocks[:, 0] + from_xor(blocks[:, 1], "core", 1)
    total = pair[count - 1]
    for d in range(count - 2, -1, -1):
        sent = total.astype(jnp.bfloat16)
        came = lax.ppermute(sent, "a", [(i, (i - 1) % count) for i in range(count)])
        total = pair[d] + came.astype(jnp.float32)
    return total


def shard_exchange(values):
    count, place = lax.axis_size("x"), lax.axis_index("x")
    came = jnp.stack([from_xor(pick(values, place ^ k), "x", k) for k in range(count)])
    return [pick(came, place ^ s) for s in range(count)]


def shard_gather(values):
    count, place = lax.axis_size("x"), lax.axis_index("x")
    came = jnp.stack([from_xor(values, "x", k) for k in range(count)])
    return jnp.concatenate([pick(came, place ^ s) for s in range(count)], axis=-1)


def rows_to_shards(values):
    count = lax.axis_size("x")
    return jnp.concatenate(
        shard_exchange(values.reshape(count, -1, values.shape[-1])), axis=-1
    )


def rows_from_shards(values):
    count = lax.axis_size("x")
    split = jnp.stack(jnp.split(values, count, axis=-1))
    return jnp.concatenate(shard_exchange(split), axis=-2)


def row_blocks(parts):
    n, s = lax.axis_size(DP), lax.axis_size("x")
    joined = jnp.concatenate([part.reshape(n, -1, part.shape[-1]) for part in parts], axis=1)
    width = joined.shape[-1]
    moved = lax.all_to_all(joined, DP, 0, 0, tiled=True)
    whole = jnp.transpose(moved, (1, 0, 2)).reshape(-1, n * width)
    return lax.ppermute(whole, ALL, [(d * s + x, x * n + d) for d in range(n) for x in range(s)])


def row_blocks_back(block):
    n, s = lax.axis_size(DP), lax.axis_size("x")
    whole = lax.ppermute(block, ALL, [(x * n + d, d * s + x) for d in range(n) for x in range(s)])
    rows, width = whole.shape[0], whole.shape[1] // n
    pieces = jnp.transpose(whole.reshape(rows, n, width), (1, 0, 2))
    return lax.all_to_all(pieces, DP, 0, 0, tiled=True)


def triple_tables(n):
    block_of = [[0] * 3 for _ in range(n)]
    round_of = [[0] * 3 for _ in range(n)]
    for i in range(n):
        for r in range(3):
            block_of[(3 * i + r) % n][r] = (3 * i + r) // n
            round_of[(3 * i + r) % n][(3 * i + r) // n] = r
    return jnp.array(block_of, jnp.int32), jnp.array(round_of, jnp.int32)


def triple_blocks(weight):
    n, s = lax.axis_size(DP), lax.axis_size("x")
    granules = weight.T.reshape(3, s, -1, weight.shape[0])
    came = jnp.stack(
        [lax.ppermute(granules[r], DP, [(i, (3 * i + r) % n) for i in range(n)]) for r in range(3)]
    )
    order = triple_tables(n)[1][lax.axis_index(DP)]
    blocks = jnp.concatenate([pick(came, order[b]) for b in range(3)], axis=1)
    return jnp.concatenate(shard_exchange(blocks), axis=-1)


def triple_blocks_back(grad):
    n, s = lax.axis_size(DP), lax.axis_size("x")
    split = jnp.stack(jnp.split(grad, s, axis=-1))
    came = [block.reshape(3, -1, block.shape[-1]) for block in shard_exchange(split)]
    blocks = jnp.concatenate(came, axis=1)
    order = triple_tables(n)[0][lax.axis_index(DP)]
    granules = [
        lax.ppermute(pick(blocks, order[r]), DP, [((3 * i + r) % n, i) for i in range(n)])
        for r in range(3)
    ]
    return jnp.concatenate(granules, axis=0).T


def team_features(vector):
    a, b, x = lax.axis_size("a"), lax.axis_size("b"), lax.axis_size("x")
    split = vector.reshape(vector.shape[0], a, b, 2, x, -1)
    split = pick(pick(split, lax.axis_index("b"), 2), lax.axis_index("x"), 3)
    place, core = lax.axis_index("a"), lax.axis_index("core")
    found = []
    for d in range(a):
        for k in range(2):
            found.append(pick(pick(split, (place - d + a) % a, 1), core ^ k, 1))
    return jnp.concatenate(found, axis=1)


def team_features_back(vector, width):
    a, b, x = lax.axis_size("a"), lax.axis_size("b"), lax.axis_size("x")
    rows = vector.shape[0]
    split = vector.reshape(rows, a, 2, -1)
    place, core = lax.axis_index("a"), lax.axis_index("core")
    ordered = []
    for i in range(a):
        for k in range(2):
            ordered.append(pick(pick(split, (place - i + a) % a, 1), core ^ k, 1))
    ordered = jnp.stack(ordered, axis=1).reshape(rows, a, 1, 2, 1, -1)
    zeros = jnp.zeros((rows, a, b, 2, x, width // (a * b * 2 * x)), vector.dtype)
    return lax.dynamic_update_slice(
        zeros, ordered, (0, 0, lax.axis_index("b"), 0, lax.axis_index("x"), 0)
    ).reshape(rows, width)


def vector_sum(terms):
    count, place = lax.axis_size("x"), lax.axis_index("x")
    split = jnp.stack(jnp.split(terms, count, axis=1))
    total = pick(split, place)
    for k in range(1, count):
        total = total + from_xor(pick(split, place ^ k), "x", k)
    for axis in DP:
        step = 1
        while step < lax.axis_size(axis):
            total = total + from_xor(total, axis, step)
            step *= 2
    return total


def adam_step(param, grad, moment, square, rate, decay):
    moment_new = beta_first * moment + (1.0 - beta_first) * grad
    square_new = beta_second * square + (1.0 - beta_second) * grad * grad
    corrected = moment_new / (1.0 - beta_first**STEP)
    spread = jnp.sqrt(square_new / (1.0 - beta_second**STEP))
    updated = param - rate * (corrected / (spread + epsilon_adam) + decay * param)
    return (updated, moment_new, square_new)


def shards(
    block_input,
    out_cotangent,
    weight_input,
    weight_output,
    weight_gate,
    weight_up,
    weight_down,
    conv_taps,
    norm_gains,
    first_input,
    first_output,
    first_gate,
    first_up,
    first_down,
    first_taps,
    first_gains,
    second_input,
    second_output,
    second_gate,
    second_up,
    second_down,
    second_taps,
    second_gains,
):
    half = jnp.bfloat16
    width = block_input.shape[1]
    ff_rows = weight_down.shape[0] // lax.axis_size(DP)

    mix_block = triple_blocks(weight_input.astype(half))
    mix_rows = mix_block.shape[0] // 3
    found = pool_gather(mix_block)
    team_in = [
        jnp.concatenate([block[mix_rows * i : mix_rows * (i + 1)] for block in found], axis=0)
        for i in range(3)
    ]
    rows = row_blocks([weight_down.astype(half), weight_output.astype(half)])
    team_out = jnp.concatenate(pool_gather(rows[ff_rows:]), axis=0)
    team_gate = jnp.concatenate(pool_gather(rows_to_shards(weight_gate.astype(half).T)), axis=0)
    team_up = jnp.concatenate(pool_gather(rows_to_shards(weight_up.astype(half).T)), axis=0)
    team_down = jnp.concatenate(pool_gather(rows[:ff_rows]), axis=0)
    vectors = shard_gather(
        jnp.concatenate([conv_taps, norm_gains], axis=0).astype(half)
    ).astype(jnp.float32)
    gains = vectors[KCONV:]
    taps = team_features(vectors[:KCONV])

    values = block_input.astype(jnp.float32)
    cotangents = team_gather(out_cotangent)
    scale_one = norm_scale(values)
    normed_one = values * scale_one
    hidden_one = team_gather((normed_one * gains[0]).astype(half))
    input_gate = times_transposed(hidden_one, team_in[0])
    output_gate = times_transposed(hidden_one, team_in[1])
    mixer_values = times_transposed(hidden_one, team_in[2])
    mixed_in = input_gate * mixer_values
    shifted = [delayed(mixed_in, step) for step in range(KCONV)]
    conv_out = taps[0] * shifted[0]
    for step in range(1, KCONV):
        conv_out = conv_out + taps[step] * shifted[step]
    gated = (output_gate * conv_out).astype(half)
    residual = values + team_sum(product(gated, team_out), jnp.float32)
    scale_two = norm_scale(residual)
    normed_two = residual * scale_two
    hidden_two = team_gather((normed_two * gains[1]).astype(half))
    gate_pre = times_transposed(hidden_two, team_gate)
    up_pre = times_transposed(hidden_two, team_up)
    act_grad = times_transposed(cotangents, team_down)
    sigmoid_gate = jax.nn.sigmoid(gate_pre)
    silu_gate = gate_pre * sigmoid_gate
    activated = (silu_gate * up_pre).astype(half)
    gate_grad = (act_grad * up_pre * sigmoid_gate * (1.0 + gate_pre * (1.0 - sigmoid_gate))).astype(
        half
    )
    up_grad = (act_grad * silu_gate).astype(half)
    hidden_two_grad = team_sum(
        product(gate_grad, team_gate) + product(up_grad, team_up), jnp.float32
    )
    block_output = (residual + team_sum(product(activated, team_down), half)).astype(half)
    gain_two_grad = jnp.sum(hidden_two_grad * normed_two, axis=0)
    residual_grad = out_cotangent.astype(jnp.float32) + norm_back(
        hidden_two_grad, normed_two, scale_two, gains[1]
    )
    residual_half = team_gather(residual_grad.astype(half))
    own_down = pool_sum(transposed_times(activated, cotangents))
    own_gate = pool_sum(transposed_times(gate_grad, hidden_two))
    own_up = pool_sum(transposed_times(up_grad, hidden_two))
    gated_grad = times_transposed(residual_half, team_out)
    conv_grad = gated_grad * output_gate
    mixed_grad = taps[0] * conv_grad
    for step in range(1, KCONV):
        mixed_grad = mixed_grad + taps[step] * advanced(conv_grad, step)
    taps_grad = jnp.stack([jnp.sum(conv_grad * shifted[step], axis=0) for step in range(KCONV)], 0)
    projected_grad = [
        (mixed_grad * mixer_values).astype(half),
        (gated_grad * conv_out).astype(half),
        (mixed_grad * input_gate).astype(half),
    ]
    hidden_one_grad = team_sum(
        product(projected_grad[0], team_in[0])
        + product(projected_grad[1], team_in[1])
        + product(projected_grad[2], team_in[2]),
        half,
    )
    pool = 2 * lax.axis_size("a")
    own_out = pool_sum(transposed_times(gated, residual_half))
    terms = [transposed_times(grad, hidden_one).reshape(pool, -1, width) for grad in projected_grad]
    own_mix = pool_sum(jnp.concatenate(terms, axis=1))
    gain_one_grad = jnp.sum(hidden_one_grad * normed_one, axis=0)
    input_gradient = residual_grad + norm_back(hidden_one_grad, normed_one, scale_one, gains[0])
    vector_terms = jnp.concatenate(
        [team_features_back(taps_grad, width), gain_one_grad[None, :], gain_two_grad[None, :]],
        axis=0,
    )
    vector_total = vector_sum(vector_terms)
    grad_taps = vector_total[:KCONV]
    grad_gains = vector_total[KCONV:]

    grad_gate = rows_from_shards(own_gate).T
    grad_up = rows_from_shards(own_up).T
    grad_input = triple_blocks_back(own_mix)
    grad_rows = row_blocks_back(jnp.concatenate([own_down, own_out], axis=0))
    grad_down = grad_rows[:, :ff_rows].reshape(weight_down.shape)
    grad_output = grad_rows[:, ff_rows:].reshape(weight_output.shape)
    params = (
        weight_input,
        weight_output,
        weight_gate,
        weight_up,
        weight_down,
        conv_taps,
        norm_gains,
    )
    grads = (grad_input, grad_output, grad_gate, grad_up, grad_down, grad_taps, grad_gains)
    firsts = (first_input, first_output, first_gate, first_up, first_down, first_taps, first_gains)
    seconds = (
        second_input,
        second_output,
        second_gate,
        second_up,
        second_down,
        second_taps,
        second_gains,
    )
    updated = []
    moments = []
    squares = []
    for index in range(7):
        rate = rate_matrix if index < 5 else rate_vector
        decay = weight_decay if index < 5 else 0.0
        result = adam_step(params[index], grads[index], firsts[index], seconds[index], rate, decay)
        updated.append(result[0])
        moments.append(result[1])
        squares.append(result[2])
    return (
        block_output,
        input_gradient,
        grads[0],
        grads[1],
        grads[2],
        grads[3],
        grads[4],
        grads[5],
        grads[6],
        updated[0],
        updated[1],
        updated[2],
        updated[3],
        updated[4],
        updated[5],
        updated[6],
        moments[0],
        moments[1],
        moments[2],
        moments[3],
        moments[4],
        moments[5],
        moments[6],
        squares[0],
        squares[1],
        squares[2],
        squares[3],
        squares[4],
        squares[5],
        squares[6],
    )


def solution(mesh):
    dp, shard = mesh.shape["dp"], mesh.shape["shard"]
    mesh = Mesh(mesh.devices.reshape(dp // 4, 2, 2, shard), ALL)
    placed = (
        P(ALL, None),
        P(ALL, None),
        P("x", DP),
        P("x", DP),
        P("x", DP),
        P("x", DP),
        P("x", DP),
        P(None, "x"),
        P(None, "x"),
        P("x", DP),
        P("x", DP),
        P("x", DP),
        P("x", DP),
        P("x", DP),
        P(None, "x"),
        P(None, "x"),
        P("x", DP),
        P("x", DP),
        P("x", DP),
        P("x", DP),
        P("x", DP),
        P(None, "x"),
        P(None, "x"),
    )
    return jax.shard_map(
        shards,
        mesh=mesh,
        in_specs=placed,
        out_specs=(
            P(ALL, None),
            P(ALL, None),
            P("x", DP),
            P("x", DP),
            P("x", DP),
            P("x", DP),
            P("x", DP),
            P(None, "x"),
            P(None, "x"),
            P("x", DP),
            P("x", DP),
            P("x", DP),
            P("x", DP),
            P("x", DP),
            P(None, "x"),
            P(None, "x"),
            P("x", DP),
            P("x", DP),
            P("x", DP),
            P("x", DP),
            P("x", DP),
            P(None, "x"),
            P(None, "x"),
            P("x", DP),
            P("x", DP),
            P("x", DP),
            P("x", DP),
            P("x", DP),
            P(None, "x"),
            P(None, "x"),
        ),
        check_vma=False,
    )
```

```python
import jax
import jax.numpy as jnp
from jax import lax
from jax.sharding import Mesh
from jax.sharding import PartitionSpec as P

KCONV = 3
LEN = 128
STEP = 10


epsilon_norm = 1e-05
epsilon_adam = 1e-08
beta_first = 0.9
beta_second = 0.95
rate_matrix = 0.01
rate_vector = 0.1
weight_decay = 0.1


def product(left, right):
    return jnp.dot(left, right, preferred_element_type=jnp.float32)


def times_transposed(left, right):
    return lax.dot_general(
        left, right, (((1,), (1,)), ((), ())), preferred_element_type=jnp.float32
    )


def transposed_times(left, right):
    return lax.dot_general(
        left, right, (((0,), (0,)), ((), ())), preferred_element_type=jnp.float32
    )


def delayed(values, steps):
    seqs = values.reshape(-1, LEN, values.shape[-1])
    padded = jnp.pad(seqs, ((0, 0), (steps, 0), (0, 0)))[:, :LEN]
    return padded.reshape(values.shape)


def advanced(values, steps):
    seqs = values.reshape(-1, LEN, values.shape[-1])
    padded = jnp.pad(seqs, ((0, 0), (0, steps), (0, 0)))[:, steps:]
    return padded.reshape(values.shape)


def norm_scale(values):
    return lax.rsqrt(jnp.mean(values * values, axis=1, keepdims=True) + epsilon_norm)


def norm_back(grad_in, normed, scale, gain):
    weighted = grad_in * gain
    return scale * (weighted - normed * jnp.mean(weighted * normed, axis=1, keepdims=True))


LINE = ("u", "w")
DP = ("u", "w", "b", "core")
RING = ("b", "x")
ALL = ("u", "w", "b", "core", "x")


def from_xor(values, axes, k):
    if k == 0:
        return values
    return lax.ppermute(values, axes, [(i, i ^ k) for i in range(lax.axis_size(axes))])


def pick(values, index, axis=0):
    return lax.dynamic_index_in_dim(values, index, axis, keepdims=False)


def xor_order(values, axis, place):
    shape, step = values.shape, 1
    while step < shape[axis]:
        split = values.reshape(shape[:axis] + (-1, 2, step) + shape[axis + 1 :])
        same = (place // step) % 2 == 0
        values = jnp.where(same, split, jnp.flip(split, axis + 1)).reshape(shape)
        step *= 2
    return values


def team_gather(values, axes):
    blocks = [from_xor(values, axes, k) for k in range(lax.axis_size(axes))]
    return jnp.concatenate(blocks, axis=0)


def team_blocks(partial, axes, wire):
    count = lax.axis_size(axes)
    blocks = partial.reshape(count, -1, partial.shape[-1])
    return [blocks[0]] + [from_xor(blocks[k].astype(wire), axes, k) for k in range(1, count)]


def added(blocks):
    total = blocks[0]
    for block in blocks[1:]:
        total = total + block.astype(jnp.float32)
    return total


def team_sum(partial, axes, wire):
    return added(team_blocks(partial, axes, wire))


def pool_gather(block, axes):
    mine = jnp.stack([from_xor(block, axes, k) for k in range(lax.axis_size(axes))])
    return jnp.stack([mine, from_xor(mine, "core", 1)])


def send_terms(pieces, axes):
    total = pieces[0]
    for k in range(1, len(pieces)):
        came = from_xor(pieces[k].astype(jnp.bfloat16), axes, k)
        total = total + came.astype(jnp.float32)
    return total


def both_cores(blocks, axis):
    core = lax.axis_index("core")
    return pick(blocks, core, axis) + from_xor(pick(blocks, 1 - core, axis), "core", 1)


def fan_matrix(gathered):
    s, b = lax.axis_size("x"), lax.axis_size("b")
    rows, part = gathered.shape[2:]
    split = gathered.reshape(2, b, s, rows, part)
    split = xor_order(xor_order(split, 0, lax.axis_index("core")), 1, lax.axis_index("b"))
    return split.transpose(1, 0, 3, 2, 4).reshape(-1, s * part)


def fan_pieces(terms):
    s, b = lax.axis_size("x"), lax.axis_size("b")
    part = terms.shape[1] // s
    pair = both_cores(terms.reshape(b, 2, -1, terms.shape[1]), 1)
    place = lax.axis_index("b")
    blocks = [pick(pair, place ^ i) for i in range(b)]
    return [blocks[i][:, k * part : (k + 1) * part] for i in range(b) for k in range(s)]


def line_matrix(gathered):
    ordered = xor_order(gathered, 0, lax.axis_index("core"))
    return jnp.swapaxes(xor_order(ordered, 1, lax.axis_index(LINE)), 0, 1)


def turned(values):
    count, place = lax.axis_size("x"), lax.axis_index("x")
    split = jnp.stack(jnp.split(values, count, axis=-1))
    return jnp.concatenate([pick(split, place ^ k) for k in range(count)], axis=-1)


def shard_exchange(values):
    count, place = lax.axis_size("x"), lax.axis_index("x")
    came = jnp.stack([from_xor(pick(values, place ^ k), "x", k) for k in range(count)])
    return [pick(came, place ^ s) for s in range(count)]


def shard_gather(values):
    count, place = lax.axis_size("x"), lax.axis_index("x")
    came = jnp.stack([from_xor(values, "x", k) for k in range(count)])
    return jnp.concatenate([pick(came, place ^ s) for s in range(count)], axis=-1)


def crossed(values, k):
    s, w, b = lax.axis_size("x"), lax.axis_size("w"), lax.axis_size("b") * 2
    pairs = [
        (((u * w + i) * b + j) * s + x, ((x * w + (i ^ k)) * b + j) * s + u)
        for u in range(s)
        for i in range(w)
        for j in range(b)
        for x in range(s)
    ]
    return lax.ppermute(values, ALL, pairs)


def cross_exchange(values):
    count, place = lax.axis_size("w"), lax.axis_index("w")
    came = jnp.stack([crossed(pick(values, place ^ k), k) for k in range(count)])
    return [pick(came, place ^ i) for i in range(count)]


def ring_exchange(values):
    count, place = lax.axis_size(RING), lax.axis_index(RING)
    came = jnp.stack([from_xor(pick(values, place ^ k), RING, k) for k in range(count)])
    return [pick(came, place ^ r) for r in range(count)]


def out_blocks(weight):
    b, s, w = lax.axis_size("b"), lax.axis_size("x"), lax.axis_size("w")
    cols = weight.shape[1]
    split = weight.T.reshape(cols, w, b, 2, s, -1).transpose(2, 4, 0, 1, 3, 5)
    came = ring_exchange(split.reshape(b * s, cols, -1))
    return jnp.stack([jnp.concatenate(came[i * s : (i + 1) * s], axis=1) for i in range(b)])


def out_blocks_back(grad):
    b, s, w = lax.axis_size("b"), lax.axis_size("x"), lax.axis_size("w")
    cols = grad.shape[1]
    split = grad.reshape(b, cols, s, -1).swapaxes(1, 2)
    came = jnp.stack(ring_exchange(split.reshape(b * s, cols, -1)))
    split = came.reshape(b, s, cols, w, 2, -1).transpose(2, 3, 0, 4, 1, 5)
    return split.reshape(cols, -1).T


def fan_order(values, back):
    s, w, b = lax.axis_size("x"), lax.axis_size("w"), lax.axis_size("b")
    x, j, core = lax.axis_index("x"), lax.axis_index("b"), lax.axis_index("core")
    rows, width = values.shape
    shape = (rows, 2, b, s, w, -1) if back else (rows, s, w, b, 2, -1)
    split = values.reshape(shape)
    places = ((core, 1), (j, 2), (x, 3)) if back else ((x, 1), (j, 3), (core, 4))
    for place, axis in places:
        split = jnp.stack(
            [pick(split, place ^ k, axis) for k in range(split.shape[axis])], axis=axis
        )
    order = (0, 3, 4, 2, 1, 5) if back else (0, 4, 3, 1, 2, 5)
    return split.transpose(order).reshape(rows, width)


def triple_tables(n):
    block_of = [[0] * 3 for _ in range(n)]
    round_of = [[0] * 3 for _ in range(n)]
    for i in range(n):
        for r in range(3):
            block_of[(3 * i + r) % n][r] = (3 * i + r) // n
            round_of[(3 * i + r) % n][(3 * i + r) // n] = r
    return jnp.array(block_of, jnp.int32), jnp.array(round_of, jnp.int32)


def triple_blocks(weight):
    n = lax.axis_size(DP)
    granules = weight.T.reshape(3, -1, weight.shape[0])
    came = jnp.stack(
        [lax.ppermute(granules[r], DP, [(i, (3 * i + r) % n) for i in range(n)]) for r in range(3)]
    )
    order = triple_tables(n)[1][lax.axis_index(DP)]
    return jnp.stack([pick(came, order[i]) for i in range(3)])


def triple_blocks_back(blocks):
    n = lax.axis_size(DP)
    order = triple_tables(n)[0][lax.axis_index(DP)]
    granules = [
        lax.ppermute(pick(blocks, order[r]), DP, [((3 * i + r) % n, i) for i in range(n)])
        for r in range(3)
    ]
    return jnp.concatenate(granules, axis=0).T


def team_features(vector):
    a, b, x = lax.axis_size(LINE), lax.axis_size("b"), lax.axis_size("x")
    split = vector.reshape(vector.shape[0], a, b, 2, x, -1)
    split = pick(pick(split, lax.axis_index("b"), 2), lax.axis_index("x"), 3)
    return split.reshape(vector.shape[0], -1)


def team_features_back(vector, width):
    a, b, x = lax.axis_size(LINE), lax.axis_size("b"), lax.axis_size("x")
    rows = vector.shape[0]
    zeros = jnp.zeros((rows, a, b, 2, x, width // (a * b * 2 * x)), vector.dtype)
    return lax.dynamic_update_slice(
        zeros,
        vector.reshape(rows, a, 1, 2, 1, -1),
        (0, 0, lax.axis_index("b"), 0, lax.axis_index("x"), 0),
    ).reshape(rows, width)


def vector_sum(terms):
    count, place = lax.axis_size("x"), lax.axis_index("x")
    split = jnp.stack(jnp.split(terms, count, axis=1))
    total = pick(split, place)
    for k in range(1, count):
        total = total + from_xor(pick(split, place ^ k), "x", k)
    for axis in (LINE, "b", "core"):
        step = 1
        while step < lax.axis_size(axis):
            total = total + from_xor(total, axis, step)
            step *= 2
    return total


def adam_step(param, grad, moment, square, rate, decay):
    moment_new = beta_first * moment + (1.0 - beta_first) * grad
    square_new = beta_second * square + (1.0 - beta_second) * grad * grad
    corrected = moment_new / (1.0 - beta_first**STEP)
    spread = jnp.sqrt(square_new / (1.0 - beta_second**STEP))
    updated = param - rate * (corrected / (spread + epsilon_adam) + decay * param)
    return (updated, moment_new, square_new)


def program(
    block_input,
    out_cotangent,
    weight_input,
    weight_output,
    weight_gate,
    weight_up,
    weight_down,
    conv_taps,
    norm_gains,
    first_input,
    first_output,
    first_gate,
    first_up,
    first_down,
    first_taps,
    first_gains,
    second_input,
    second_output,
    second_gate,
    second_up,
    second_down,
    second_taps,
    second_gains,
):
    half = jnp.bfloat16
    full = jnp.float32
    width = block_input.shape[1]
    shard_count = lax.axis_size("x")

    vectors = shard_gather(jnp.concatenate([conv_taps, norm_gains], axis=0).astype(half)).astype(full)
    gains = vectors[KCONV:]
    taps = team_features(vectors[:KCONV])
    values = block_input.astype(full)
    scale_one = norm_scale(values)
    normed_one = values * scale_one
    hidden_one = team_gather((normed_one * gains[0]).astype(half), RING)

    triple = triple_blocks(weight_input.astype(half))
    mix_split = triple.reshape(3, shard_count, -1, triple.shape[-1])
    mix_block = jnp.concatenate(shard_exchange(jnp.swapaxes(mix_split, 0, 1)), axis=-1)
    mix_pool = pool_gather(mix_block, LINE)
    mix_pool = line_matrix(mix_pool)
    team_mix = [mix_pool[:, :, i].reshape(-1, width) for i in range(3)]
    out_block = out_blocks(weight_output.astype(half))
    out_pool = pool_gather(out_block, LINE)
    team_out = jnp.swapaxes(line_matrix(out_pool), 1, 2).reshape(width, -1)
    fan_block = jnp.stack([weight_gate.astype(half).T, weight_up.astype(half).T])
    fan_block = lax.optimization_barrier(fan_block)
    down = weight_down.astype(half).T
    fan_pool = pool_gather(fan_block, RING)
    team_gate = fan_matrix(fan_pool[:, :, 0])
    team_up = fan_matrix(fan_pool[:, :, 1])
    down_split = jnp.stack(jnp.split(down, lax.axis_size("w"), axis=1))
    down_block = jnp.stack(cross_exchange(down_split))
    team_down = pool_gather(down_block, RING).reshape(width, -1)

    input_gate = times_transposed(hidden_one, team_mix[0])
    output_gate = times_transposed(hidden_one, team_mix[1])
    mixer_values = times_transposed(hidden_one, team_mix[2])
    mixed_in = input_gate * mixer_values
    shifted = [delayed(mixed_in, step) for step in range(KCONV)]
    conv_out = taps[0] * shifted[0]
    for step in range(1, KCONV):
        conv_out = conv_out + taps[step] * shifted[step]
    gated = (output_gate * conv_out).astype(half)
    mixed_terms = times_transposed(gated, team_out)
    residual = values + team_sum(mixed_terms, RING, full)
    scale_two = norm_scale(residual)
    normed_two = residual * scale_two
    hidden_two = team_gather(turned((normed_two * gains[1]).astype(half)), LINE)
    cotangents = team_gather(fan_order(out_cotangent, False), LINE)
    act_grad = product(cotangents, team_down)
    gate_pre = times_transposed(hidden_two, team_gate)
    up_pre = times_transposed(hidden_two, team_up)
    sigmoid_gate = jax.nn.sigmoid(gate_pre)
    silu_gate = gate_pre * sigmoid_gate
    activated = (silu_gate * up_pre).astype(half)
    gate_grad = (act_grad * up_pre * sigmoid_gate * (1.0 + gate_pre * (1.0 - sigmoid_gate))).astype(
        half
    )
    up_grad = (act_grad * silu_gate).astype(half)
    hidden_two_terms = product(gate_grad, team_gate) + product(up_grad, team_up)
    hidden_two_grad = turned(team_sum(hidden_two_terms, LINE, full))
    count = lax.axis_size(RING)
    down_terms = transposed_times(cotangents, activated)
    gate_terms = transposed_times(gate_grad, hidden_two)
    up_terms = transposed_times(up_grad, hidden_two)
    down_terms = down_terms.reshape(2, -1, activated.shape[1])
    down_pair = down_terms[0] + from_xor(down_terms[1], "core", 1)
    own_down = send_terms(list(down_pair.reshape(count, -1, activated.shape[1])), RING)
    fan_terms = [fan_pieces(gate_terms), fan_pieces(up_terms)]
    own_fan = send_terms([jnp.stack(pair) for pair in zip(*fan_terms)], RING)
    down_split = own_down.reshape(lax.axis_size("w"), -1, own_down.shape[-1])
    down_split = jnp.concatenate(cross_exchange(down_split.astype(half)), axis=1)
    grad_down = down_split.T.astype(full)
    grad_gate = own_fan[0].T
    grad_up = own_fan[1].T
    gain_two_grad = jnp.sum(hidden_two_grad * normed_two, axis=0)
    residual_grad = out_cotangent.astype(full) + norm_back(
        hidden_two_grad, normed_two, scale_two, gains[1]
    )
    residual_half = team_gather(residual_grad.astype(half), RING)
    gated_grad = product(residual_half, team_out)
    conv_grad = gated_grad * output_gate
    mixed_grad = taps[0] * conv_grad
    for step in range(1, KCONV):
        mixed_grad = mixed_grad + taps[step] * advanced(conv_grad, step)
    taps_grad = jnp.stack([jnp.sum(conv_grad * shifted[step], axis=0) for step in range(KCONV)], 0)
    projected_grad = [
        (mixed_grad * mixer_values).astype(half),
        (gated_grad * conv_out).astype(half),
        (mixed_grad * input_gate).astype(half),
    ]
    hidden_one_terms = (
        product(projected_grad[0], team_mix[0])
        + product(projected_grad[1], team_mix[1])
        + product(projected_grad[2], team_mix[2])
    )
    hidden_one_grad = team_sum(hidden_one_terms, RING, half)
    out_terms = lax.optimization_barrier(times_transposed(activated, team_down))
    late_came = team_blocks(out_terms, LINE, half)
    late_came, residual, hidden_one_grad = lax.optimization_barrier(
        (late_came, residual, hidden_one_grad)
    )
    block_output = (residual + fan_order(added(late_came), True)).astype(half)
    line, place = lax.axis_size(LINE), lax.axis_index(LINE)
    terms = [
        transposed_times(grad, hidden_one).reshape(line, 2, -1, width) for grad in projected_grad
    ]
    pair = both_cores(jnp.stack(terms, axis=2), 1)
    own_mix = send_terms([pick(pair, place ^ k) for k in range(line)], LINE)
    out_terms = transposed_times(residual_half, gated)
    out_terms = out_terms.reshape(line, lax.axis_size("b"), 2, -1, out_terms.shape[-1])
    pair = both_cores(out_terms, 2)
    own_out = send_terms([pick(pair, place ^ k) for k in range(line)], LINE)
    grad_output = out_blocks_back(own_out)
    gain_one_grad = jnp.sum(hidden_one_grad * normed_one, axis=0)
    input_gradient = residual_grad + norm_back(hidden_one_grad, normed_one, scale_one, gains[0])
    vector_terms = jnp.concatenate(
        [team_features_back(taps_grad, width), gain_one_grad[None, :], gain_two_grad[None, :]],
        axis=0,
    )
    mix_split = jnp.stack(jnp.split(own_mix, shard_count, axis=-1))
    grad_input = triple_blocks_back(jnp.concatenate(shard_exchange(mix_split), axis=1))
    vector_total = vector_sum(vector_terms)
    grad_taps = vector_total[:KCONV]
    grad_gains = vector_total[KCONV:]
    params = (
        weight_input,
        weight_output,
        weight_gate,
        weight_up,
        weight_down,
        conv_taps,
        norm_gains,
    )
    grads = (grad_input, grad_output, grad_gate, grad_up, grad_down, grad_taps, grad_gains)
    firsts = (first_input, first_output, first_gate, first_up, first_down, first_taps, first_gains)
    seconds = (
        second_input,
        second_output,
        second_gate,
        second_up,
        second_down,
        second_taps,
        second_gains,
    )
    updated = []
    moments = []
    squares = []
    for index in range(7):
        rate = rate_matrix if index < 5 else rate_vector
        decay = weight_decay if index < 5 else 0.0
        result = adam_step(params[index], grads[index], firsts[index], seconds[index], rate, decay)
        updated.append(result[0])
        moments.append(result[1])
        squares.append(result[2])
    return (
        block_output,
        input_gradient,
        grads[0],
        grads[1],
        grads[2],
        grads[3],
        grads[4],
        grads[5],
        grads[6],
        updated[0],
        updated[1],
        updated[2],
        updated[3],
        updated[4],
        updated[5],
        updated[6],
        moments[0],
        moments[1],
        moments[2],
        moments[3],
        moments[4],
        moments[5],
        moments[6],
        squares[0],
        squares[1],
        squares[2],
        squares[3],
        squares[4],
        squares[5],
        squares[6],
    )


def solution(mesh):
    dp, shard = mesh.shape["dp"], mesh.shape["shard"]
    mesh = Mesh(mesh.devices.reshape(shard, dp // (4 * shard), 2, 2, shard), ALL)
    placed = (
        P(ALL, None),
        P(ALL, None),
        P("x", DP),
        P("x", DP),
        P("x", DP),
        P("x", DP),
        P("x", DP),
        P(None, "x"),
        P(None, "x"),
        P("x", DP),
        P("x", DP),
        P("x", DP),
        P("x", DP),
        P("x", DP),
        P(None, "x"),
        P(None, "x"),
        P("x", DP),
        P("x", DP),
        P("x", DP),
        P("x", DP),
        P("x", DP),
        P(None, "x"),
        P(None, "x"),
    )
    return jax.shard_map(
        program,
        mesh=mesh,
        in_specs=placed,
        out_specs=(
            P(ALL, None),
            P(ALL, None),
            P("x", DP),
            P("x", DP),
            P("x", DP),
            P("x", DP),
            P("x", DP),
            P(None, "x"),
            P(None, "x"),
            P("x", DP),
            P("x", DP),
            P("x", DP),
            P("x", DP),
            P("x", DP),
            P(None, "x"),
            P(None, "x"),
            P("x", DP),
            P("x", DP),
            P("x", DP),
            P("x", DP),
            P("x", DP),
            P(None, "x"),
            P(None, "x"),
            P("x", DP),
            P("x", DP),
            P("x", DP),
            P("x", DP),
            P("x", DP),
            P(None, "x"),
            P(None, "x"),
        ),
        check_vma=False,
    )
```

```python
import jax
import jax.numpy as jnp
from jax import lax
from jax.sharding import Mesh
from jax.sharding import PartitionSpec as P

KCONV = 3
LEN = 128
STEP = 10


epsilon_norm = 1e-05
epsilon_adam = 1e-08
beta_first = 0.9
beta_second = 0.95
rate_matrix = 0.01
rate_vector = 0.1
weight_decay = 0.1


def product(left, right):
    return jnp.dot(left, right, preferred_element_type=jnp.float32)


def times_transposed(left, right):
    return lax.dot_general(
        left, right, (((1,), (1,)), ((), ())), preferred_element_type=jnp.float32
    )


def transposed_times(left, right):
    return lax.dot_general(
        left, right, (((0,), (0,)), ((), ())), preferred_element_type=jnp.float32
    )


def delayed(values, steps):
    seqs = values.reshape(-1, LEN, values.shape[-1])
    padded = jnp.pad(seqs, ((0, 0), (steps, 0), (0, 0)))[:, :LEN]
    return padded.reshape(values.shape)


def advanced(values, steps):
    seqs = values.reshape(-1, LEN, values.shape[-1])
    padded = jnp.pad(seqs, ((0, 0), (0, steps), (0, 0)))[:, steps:]
    return padded.reshape(values.shape)


def norm_scale(values):
    return lax.rsqrt(jnp.mean(values * values, axis=1, keepdims=True) + epsilon_norm)


def norm_back(grad_in, normed, scale, gain):
    weighted = grad_in * gain
    return scale * (weighted - normed * jnp.mean(weighted * normed, axis=1, keepdims=True))


X = "x"
B = "b"
W = "w"
CORE = "core"
LINE = ("u", "w")
DP = ("u", "w", "b", "core")
RING = ("b", "x")
ALL = ("u", "w", "b", "core", "x")


TOKENS = P(ALL, None)
MATRIX = P("x", DP)
VECTOR = P(None, "x")


def from_xor(values, axes, k):
    if k == 0:
        return values
    return lax.ppermute(values, axes, [(i, i ^ k) for i in range(lax.axis_size(axes))])


def pick(values, index, axis=0):
    return lax.dynamic_index_in_dim(values, index, axis, keepdims=False)


def xor_order(values, axis, place):
    shape, step = values.shape, 1
    while step < shape[axis]:
        split = values.reshape(shape[:axis] + (-1, 2, step) + shape[axis + 1 :])
        same = (place // step) % 2 == 0
        values = jnp.where(same, split, jnp.flip(split, axis + 1)).reshape(shape)
        step *= 2
    return values


def team_gather(values, axes):
    blocks = [from_xor(values, axes, k) for k in range(lax.axis_size(axes))]
    return jnp.concatenate(blocks, axis=0)


def team_blocks(partial, axes, wire):
    count = lax.axis_size(axes)
    blocks = partial.reshape(count, -1, partial.shape[-1])
    return [blocks[0]] + [from_xor(blocks[k].astype(wire), axes, k) for k in range(1, count)]


def added(blocks):
    total = blocks[0]
    for block in blocks[1:]:
        total = total + block.astype(jnp.float32)
    return total


def team_sum(partial, axes, wire):
    return added(team_blocks(partial, axes, wire))


def pool_gather(block, axes):
    mine = jnp.stack([from_xor(block, axes, k) for k in range(lax.axis_size(axes))])
    return jnp.stack([mine, from_xor(mine, CORE, 1)])


def send_terms(pieces, axes):
    total = pieces[0]
    for k in range(1, len(pieces)):
        came = from_xor(pieces[k].astype(jnp.bfloat16), axes, k)
        total = total + came.astype(jnp.float32)
    return total


def both_cores(blocks, axis):
    core = lax.axis_index(CORE)
    return pick(blocks, core, axis) + from_xor(pick(blocks, 1 - core, axis), CORE, 1)


def fan_matrix(gathered):
    s, b = lax.axis_size(X), lax.axis_size(B)
    rows, part = gathered.shape[2:]
    split = gathered.reshape(2, b, s, rows, part)
    split = xor_order(xor_order(split, 0, lax.axis_index(CORE)), 1, lax.axis_index(B))
    return split.transpose(1, 0, 3, 2, 4).reshape(-1, s * part)


def fan_pieces(terms):
    s, b = lax.axis_size(X), lax.axis_size(B)
    part = terms.shape[1] // s
    pair = both_cores(terms.reshape(b, 2, -1, terms.shape[1]), 1)
    place = lax.axis_index(B)
    blocks = [pick(pair, place ^ i) for i in range(b)]
    return [blocks[i][:, k * part : (k + 1) * part] for i in range(b) for k in range(s)]


def line_matrix(gathered):
    ordered = xor_order(gathered, 0, lax.axis_index(CORE))
    return jnp.swapaxes(xor_order(ordered, 1, lax.axis_index(LINE)), 0, 1)


def turned(values):
    count, place = lax.axis_size(X), lax.axis_index(X)
    split = jnp.stack(jnp.split(values, count, axis=-1))
    return jnp.concatenate([pick(split, place ^ k) for k in range(count)], axis=-1)


def shard_exchange(values):
    count, place = lax.axis_size(X), lax.axis_index(X)
    came = jnp.stack([from_xor(pick(values, place ^ k), "x", k) for k in range(count)])
    return [pick(came, place ^ s) for s in range(count)]


def shard_gather(values):
    count, place = lax.axis_size(X), lax.axis_index(X)
    came = jnp.stack([from_xor(values, "x", k) for k in range(count)])
    return jnp.concatenate([pick(came, place ^ s) for s in range(count)], axis=-1)


def crossed(values, k):
    s, w, b = lax.axis_size(X), lax.axis_size(W), lax.axis_size(B) * 2
    pairs = [
        (((u * w + i) * b + j) * s + x, ((x * w + (i ^ k)) * b + j) * s + u)
        for u in range(s)
        for i in range(w)
        for j in range(b)
        for x in range(s)
    ]
    return lax.ppermute(values, ALL, pairs)


def cross_exchange(values):
    count, place = lax.axis_size(W), lax.axis_index(W)
    came = jnp.stack([crossed(pick(values, place ^ k), k) for k in range(count)])
    return [pick(came, place ^ i) for i in range(count)]


def ring_exchange(values):
    count, place = lax.axis_size(RING), lax.axis_index(RING)
    came = jnp.stack([from_xor(pick(values, place ^ k), RING, k) for k in range(count)])
    return [pick(came, place ^ r) for r in range(count)]


def out_blocks(weight):
    b, s, w = lax.axis_size(B), lax.axis_size(X), lax.axis_size(W)
    cols = weight.shape[1]
    split = weight.T.reshape(cols, w, b, 2, s, -1).transpose(2, 4, 0, 1, 3, 5)
    came = ring_exchange(split.reshape(b * s, cols, -1))
    return jnp.stack([jnp.concatenate(came[i * s : (i + 1) * s], axis=1) for i in range(b)])


def out_blocks_back(grad):
    b, s, w = lax.axis_size(B), lax.axis_size(X), lax.axis_size(W)
    cols = grad.shape[1]
    split = grad.reshape(b, cols, s, -1).swapaxes(1, 2)
    came = jnp.stack(ring_exchange(split.reshape(b * s, cols, -1)))
    split = came.reshape(b, s, cols, w, 2, -1).transpose(2, 3, 0, 4, 1, 5)
    return split.reshape(cols, -1).T


def fan_order(values, back):
    s, w, b = lax.axis_size(X), lax.axis_size(W), lax.axis_size(B)
    x, j, core = lax.axis_index(X), lax.axis_index(B), lax.axis_index(CORE)
    rows, width = values.shape
    shape = (rows, 2, b, s, w, -1) if back else (rows, s, w, b, 2, -1)
    split = values.reshape(shape)
    places = ((core, 1), (j, 2), (x, 3)) if back else ((x, 1), (j, 3), (core, 4))
    for place, axis in places:
        split = jnp.stack(
            [pick(split, place ^ k, axis) for k in range(split.shape[axis])], axis=axis
        )
    order = (0, 3, 4, 2, 1, 5) if back else (0, 4, 3, 1, 2, 5)
    return split.transpose(order).reshape(rows, width)


def triple_tables(n):
    block_of = [[0] * 3 for _ in range(n)]
    round_of = [[0] * 3 for _ in range(n)]
    for i in range(n):
        for r in range(3):
            block_of[(3 * i + r) % n][r] = (3 * i + r) // n
            round_of[(3 * i + r) % n][(3 * i + r) // n] = r
    return jnp.array(block_of, jnp.int32), jnp.array(round_of, jnp.int32)


def triple_blocks(weight):
    n = lax.axis_size(DP)
    granules = weight.T.reshape(3, -1, weight.shape[0])
    came = jnp.stack(
        [lax.ppermute(granules[r], DP, [(i, (3 * i + r) % n) for i in range(n)]) for r in range(3)]
    )
    order = triple_tables(n)[1][lax.axis_index(DP)]
    return jnp.stack([pick(came, order[i]) for i in range(3)])


def triple_blocks_back(blocks):
    n = lax.axis_size(DP)
    order = triple_tables(n)[0][lax.axis_index(DP)]
    granules = [
        lax.ppermute(pick(blocks, order[r]), DP, [((3 * i + r) % n, i) for i in range(n)])
        for r in range(3)
    ]
    return jnp.concatenate(granules, axis=0).T


def team_features(vector):
    a, b, x = lax.axis_size(LINE), lax.axis_size(B), lax.axis_size(X)
    split = vector.reshape(vector.shape[0], a, b, 2, x, -1)
    split = pick(pick(split, lax.axis_index(B), 2), lax.axis_index(X), 3)
    return split.reshape(vector.shape[0], -1)


def team_features_back(vector, width):
    a, b, x = lax.axis_size(LINE), lax.axis_size(B), lax.axis_size(X)
    rows = vector.shape[0]
    zeros = jnp.zeros((rows, a, b, 2, x, width // (a * b * 2 * x)), vector.dtype)
    return lax.dynamic_update_slice(
        zeros,
        vector.reshape(rows, a, 1, 2, 1, -1),
        (0, 0, lax.axis_index(B), 0, lax.axis_index(X), 0),
    ).reshape(rows, width)


def vector_sum(terms):
    count, place = lax.axis_size(X), lax.axis_index(X)
    split = jnp.stack(jnp.split(terms, count, axis=1))
    total = pick(split, place)
    for k in range(1, count):
        total = total + from_xor(pick(split, place ^ k), "x", k)
    for axis in (LINE, "b", "core"):
        step = 1
        while step < lax.axis_size(axis):
            total = total + from_xor(total, axis, step)
            step *= 2
    return total


def adam_step(param, grad, moment, square, rate, decay):
    moment_new = beta_first * moment + (1.0 - beta_first) * grad
    square_new = beta_second * square + (1.0 - beta_second) * grad * grad
    corrected = moment_new / (1.0 - beta_first**STEP)
    spread = jnp.sqrt(square_new / (1.0 - beta_second**STEP))
    updated = param - rate * (corrected / (spread + epsilon_adam) + decay * param)
    return (updated, moment_new, square_new)


def program(
    block_input,
    out_cotangent,
    weight_input,
    weight_output,
    weight_gate,
    weight_up,
    weight_down,
    conv_taps,
    norm_gains,
    first_input,
    first_output,
    first_gate,
    first_up,
    first_down,
    first_taps,
    first_gains,
    second_input,
    second_output,
    second_gate,
    second_up,
    second_down,
    second_taps,
    second_gains,
):
    half = jnp.bfloat16
    full = jnp.float32
    width = block_input.shape[1]
    shard_count = lax.axis_size(X)

    vectors = shard_gather(jnp.concatenate([conv_taps, norm_gains], axis=0).astype(half)).astype(full)
    gains = vectors[KCONV:]
    taps = team_features(vectors[:KCONV])
    values = block_input.astype(full)
    scale_one = norm_scale(values)
    normed_one = values * scale_one
    hidden_one = team_gather((normed_one * gains[0]).astype(half), RING)

    triple = triple_blocks(weight_input.astype(half))
    mix_split = triple.reshape(3, shard_count, -1, triple.shape[-1])
    mix_block = jnp.concatenate(shard_exchange(jnp.swapaxes(mix_split, 0, 1)), axis=-1)
    mix_pool = pool_gather(mix_block, LINE)
    mix_pool = line_matrix(mix_pool)
    team_mix = [mix_pool[:, :, i].reshape(-1, width) for i in range(3)]
    out_block = out_blocks(weight_output.astype(half))
    out_pool = pool_gather(out_block, LINE)
    team_out = jnp.swapaxes(line_matrix(out_pool), 1, 2).reshape(width, -1)
    fan_block = jnp.stack([weight_gate.astype(half).T, weight_up.astype(half).T])
    fan_block = lax.optimization_barrier(fan_block)
    down = weight_down.astype(half).T
    fan_pool = pool_gather(fan_block, RING)
    team_gate = fan_matrix(fan_pool[:, :, 0])
    team_up = fan_matrix(fan_pool[:, :, 1])
    down_split = jnp.stack(jnp.split(down, lax.axis_size(W), axis=1))
    down_block = jnp.stack(cross_exchange(down_split))
    down_block = lax.optimization_barrier(down_block)
    team_down = pool_gather(down_block, RING).reshape(width, -1)

    input_gate = times_transposed(hidden_one, team_mix[0])
    output_gate = times_transposed(hidden_one, team_mix[1])
    mixer_values = times_transposed(hidden_one, team_mix[2])
    mixed_in = input_gate * mixer_values
    shifted = [delayed(mixed_in, step) for step in range(KCONV)]
    conv_out = taps[0] * shifted[0]
    for step in range(1, KCONV):
        conv_out = conv_out + taps[step] * shifted[step]
    gated = (output_gate * conv_out).astype(half)
    mixed_terms = times_transposed(gated, team_out)
    residual = values + team_sum(mixed_terms, RING, full)
    scale_two = norm_scale(residual)
    normed_two = residual * scale_two
    hidden_two = team_gather(turned((normed_two * gains[1]).astype(half)), LINE)
    cotangents = team_gather(fan_order(out_cotangent, False), LINE)
    act_grad = product(cotangents, team_down)
    gate_pre = times_transposed(hidden_two, team_gate)
    up_pre = times_transposed(hidden_two, team_up)
    sigmoid_gate = jax.nn.sigmoid(gate_pre)
    silu_gate = gate_pre * sigmoid_gate
    activated = (silu_gate * up_pre).astype(half)
    gate_grad = (act_grad * up_pre * sigmoid_gate * (1.0 + gate_pre * (1.0 - sigmoid_gate))).astype(
        half
    )
    up_grad = (act_grad * silu_gate).astype(half)
    hidden_two_terms = product(gate_grad, team_gate) + product(up_grad, team_up)
    hidden_two_grad = turned(team_sum(hidden_two_terms, LINE, full))
    count = lax.axis_size(RING)
    down_terms = transposed_times(cotangents, activated)
    gate_terms = transposed_times(gate_grad, hidden_two)
    up_terms = transposed_times(up_grad, hidden_two)
    down_terms = down_terms.reshape(2, -1, activated.shape[1])
    down_pair = down_terms[0] + from_xor(down_terms[1], CORE, 1)
    own_down = send_terms(list(down_pair.reshape(count, -1, activated.shape[1])), RING)
    fan_terms = [fan_pieces(gate_terms), fan_pieces(up_terms)]
    own_fan = send_terms([jnp.stack(pair) for pair in zip(*fan_terms)], RING)
    down_split = own_down.reshape(lax.axis_size(W), -1, own_down.shape[-1])
    down_split = jnp.concatenate(cross_exchange(down_split.astype(half)), axis=1)
    grad_down = down_split.T.astype(full)
    grad_gate = own_fan[0].T
    grad_up = own_fan[1].T
    gain_two_grad = jnp.sum(hidden_two_grad * normed_two, axis=0)
    residual_grad = out_cotangent.astype(full) + norm_back(
        hidden_two_grad, normed_two, scale_two, gains[1]
    )
    residual_half = team_gather(residual_grad.astype(half), RING)
    gated_grad = product(residual_half, team_out)
    conv_grad = gated_grad * output_gate
    mixed_grad = taps[0] * conv_grad
    for step in range(1, KCONV):
        mixed_grad = mixed_grad + taps[step] * advanced(conv_grad, step)
    taps_grad = jnp.stack([jnp.sum(conv_grad * shifted[step], axis=0) for step in range(KCONV)], 0)
    projected_grad = [
        (mixed_grad * mixer_values).astype(half),
        (gated_grad * conv_out).astype(half),
        (mixed_grad * input_gate).astype(half),
    ]
    hidden_one_terms = (
        product(projected_grad[0], team_mix[0])
        + product(projected_grad[1], team_mix[1])
        + product(projected_grad[2], team_mix[2])
    )
    one_came = team_blocks(hidden_one_terms, RING, half)
    hidden_one_grad = added(one_came)
    out_terms = lax.optimization_barrier(times_transposed(activated, team_down))
    late_came = team_blocks(out_terms, LINE, half)
    late_came, residual, hidden_one_grad = lax.optimization_barrier(
        (late_came, residual, hidden_one_grad)
    )
    block_output = (residual + fan_order(added(late_came), True)).astype(half)
    line, place = lax.axis_size(LINE), lax.axis_index(LINE)
    terms = [
        transposed_times(grad, hidden_one).reshape(line, 2, -1, width) for grad in projected_grad
    ]
    pair = both_cores(jnp.stack(terms, axis=2), 1)
    own_mix = send_terms([pick(pair, place ^ k) for k in range(line)], LINE)
    out_terms = transposed_times(residual_half, gated)
    out_terms = out_terms.reshape(line, lax.axis_size(B), 2, -1, out_terms.shape[-1])
    pair = both_cores(out_terms, 2)
    own_out = send_terms([pick(pair, place ^ k) for k in range(line)], LINE)
    grad_output = out_blocks_back(own_out)
    gain_one_grad = jnp.sum(hidden_one_grad * normed_one, axis=0)
    input_gradient = residual_grad + norm_back(hidden_one_grad, normed_one, scale_one, gains[0])
    vector_terms = jnp.concatenate(
        [team_features_back(taps_grad, width), gain_one_grad[None, :], gain_two_grad[None, :]],
        axis=0,
    )
    mix_split = jnp.stack(jnp.split(own_mix, shard_count, axis=-1))
    mix_grad = jnp.concatenate(shard_exchange(mix_split), axis=1)
    grad_input = triple_blocks_back(mix_grad)
    vector_total = vector_sum(vector_terms)
    grad_taps = vector_total[:KCONV]
    grad_gains = vector_total[KCONV:]
    params = (
        weight_input,
        weight_output,
        weight_gate,
        weight_up,
        weight_down,
        conv_taps,
        norm_gains,
    )
    grads = (grad_input, grad_output, grad_gate, grad_up, grad_down, grad_taps, grad_gains)
    firsts = (first_input, first_output, first_gate, first_up, first_down, first_taps, first_gains)
    seconds = (
        second_input,
        second_output,
        second_gate,
        second_up,
        second_down,
        second_taps,
        second_gains,
    )
    updated = []
    moments = []
    squares = []
    for index in range(7):
        rate = rate_matrix if index < 5 else rate_vector
        decay = weight_decay if index < 5 else 0.0
        result = adam_step(params[index], grads[index], firsts[index], seconds[index], rate, decay)
        updated.append(result[0])
        moments.append(result[1])
        squares.append(result[2])
    return (
        block_output,
        input_gradient,
        grads[0],
        grads[1],
        grads[2],
        grads[3],
        grads[4],
        grads[5],
        grads[6],
        updated[0],
        updated[1],
        updated[2],
        updated[3],
        updated[4],
        updated[5],
        updated[6],
        moments[0],
        moments[1],
        moments[2],
        moments[3],
        moments[4],
        moments[5],
        moments[6],
        squares[0],
        squares[1],
        squares[2],
        squares[3],
        squares[4],
        squares[5],
        squares[6],
    )


def solution(mesh):
    dp, shard = mesh.shape["dp"], mesh.shape["shard"]
    mesh = Mesh(mesh.devices.reshape(shard, dp // (4 * shard), 2, 2, shard), ALL)
    placed = (
        TOKENS,
        TOKENS,
        MATRIX,
        MATRIX,
        MATRIX,
        MATRIX,
        MATRIX,
        VECTOR,
        VECTOR,
        MATRIX,
        MATRIX,
        MATRIX,
        MATRIX,
        MATRIX,
        VECTOR,
        VECTOR,
        MATRIX,
        MATRIX,
        MATRIX,
        MATRIX,
        MATRIX,
        VECTOR,
        VECTOR,
    )
    return jax.shard_map(
        program,
        mesh=mesh,
        in_specs=placed,
        out_specs=(
            TOKENS,
            TOKENS,
            MATRIX,
            MATRIX,
            MATRIX,
            MATRIX,
            MATRIX,
            VECTOR,
            VECTOR,
            MATRIX,
            MATRIX,
            MATRIX,
            MATRIX,
            MATRIX,
            VECTOR,
            VECTOR,
            MATRIX,
            MATRIX,
            MATRIX,
            MATRIX,
            MATRIX,
            VECTOR,
            VECTOR,
            MATRIX,
            MATRIX,
            MATRIX,
            MATRIX,
            MATRIX,
            VECTOR,
            VECTOR,
        ),
        check_vma=False,
    )
```
